32 devices in a mesh: group: 4 (over z), row: 2 (over x), col: 4 (over y, core).
Axes of the slice: x: 2, y: 2, z: 4, core: 2. Of those that a mesh axis runs over, the one named last changes fastest.
Arguments:
- child_front: float32 [4, 4, 4, 128, 8, 2, 128], P('group', None, 'col', None, None, 'row'), as said below
- top_front: float32 [12, 4, 4, 32, 24, 2, 128], P(None, 'col', 'group', None, None, 'row'), as said below
- block_map: int32 [4, 8], replicated, may hold values from 0 to 47, as said below
- pivots: int32 [4], P('group'), may hold values from 512 to 1024, as said below
- noise: float32 [4, 1024], P('group'), may hold values from -6 to 6
- top_sample: float32 [6144], replicated, may hold values from -12 to 12
Outputs:
- top_out: float32 [12, 4, 4, 32, 24, 2, 128], P(None, 'col', 'group', None, None, 'row')
- child_sample: float32 [4, 1024], P('group')
The draws below stay inside these ranges and needn't reach their ends.
Inputs may be any that keep to these rules, and one draw needn't show every extreme that they name: `child_front`: each child front is symmetric positive definite. `top_front`: symmetric positive definite. block_map[g, u] mod 8 equals u; the entries of one row are distinct. `pivots`: A multiple of 128; some child has 1024.
All inputs are finite; a program needn't handle non-finite values.
Results may differ from the reference program's by a relative error of at most 0.00015.
Values sent between devices are 32-bit elements; how exact they have to be, the bound alone decides.
A program may use at most 64 MiB of HBM per device.

```python
import functools
import math
import jax
import jax.numpy as jnp
from jax import lax

BS = 128
CYCLE = 8
PC = 1024
UC = 1024
FP = 6144
FC = 2048
GROUPS = 4
N_GROUP = 4
N_ROW = 2
N_COL = 4


def positive_matrix(key, matrix_order):
    key_raw = jax.random.fold_in(key, 0)
    key_diagonal = jax.random.fold_in(key, 1)
    key_place = jax.random.fold_in(key, 3)
    raw = jax.random.normal(key_raw, (matrix_order, matrix_order), jnp.float32)
    coupling = (raw + raw.T) * (1.0 / math.sqrt(2.0 * matrix_order))
    diagonal = jax.random.uniform(key_diagonal, (matrix_order,), jnp.float32, 3.0, 5.0)
    places = jax.random.uniform(key_place, (2, matrix_order), jnp.float32, 0.0, 1.0)
    across = places[0][:, None] - places[0][None, :]
    along = places[1][:, None] - places[1][None, :]
    distance = jnp.sqrt(across * across + along * along)
    reach = 0.3
    kernel = 0.5 * jnp.exp(-distance / reach)
    matrix = coupling + kernel + jnp.diag(diagonal)
    return matrix


def draw_child_front(key, part):
    keys = jax.random.split(jax.random.fold_in(key, 11), GROUPS)
    fronts = jax.vmap(functools.partial(positive_matrix, matrix_order=FC))(keys)
    return fronts.reshape(GROUPS, FC // (BS * N_COL), N_COL, BS, FC // (BS * N_ROW), N_ROW, BS).astype(jnp.float32)


def draw_top_front(key, part):
    matrix = positive_matrix(jax.random.fold_in(key, 12), FP)
    return matrix.reshape(FP // (BS * N_COL), N_COL, N_GROUP, BS // N_GROUP, FP // (BS * N_ROW), N_ROW, BS).astype(jnp.float32)


def draw_block_map(key, part):
    shifts = jax.random.randint(jax.random.fold_in(key, 13), (GROUPS, UC // BS), 0, FP // (CYCLE * BS))
    places = jnp.arange(UC // BS, dtype=jnp.int32) % CYCLE
    return (shifts * CYCLE + places[None, :]).astype(jnp.int32)


def draw_pivots(key, part):
    key_count, key_full = jax.random.split(jax.random.fold_in(key, 14))
    counts = jax.random.randint(key_count, (GROUPS,), PC // (2 * BS), PC // BS + 1) * BS
    fullest = jax.random.randint(key_full, (), 0, GROUPS)
    return jnp.where(jnp.arange(GROUPS) == fullest, PC, counts).astype(jnp.int32)


def block_scale(own_key, shape, shards, smallest, top_value):
    gain, own = 1.0, jax.random.fold_in(own_key, 6)
    for axis_at, parts in shards:
        steps = jnp.exp(jax.random.uniform(jax.random.fold_in(own, axis_at), (parts,), jnp.float32, smallest / len(shards), top_value / len(shards)))
        gain = gain * jnp.repeat(steps, shape[axis_at] // parts).reshape([-1 if axis == axis_at else 1 for axis in range(len(shape))])
    return gain


def bell_draw(key, shape, spread, bound, shards=(), kind=jnp.bfloat16):
    loudness = block_scale(key, shape, shards, -0.22, 0.18) if shards else 1.0
    result = jax.random.normal(key, shape, jnp.float32) * spread * loudness
    return jnp.minimum(jnp.maximum(result, -bound), bound).astype(kind)


def setup_inputs(seed: int = 0) -> dict:
    splits = jax.random.split(jax.random.key(seed), 7)
    return {
        "child_front": draw_child_front(jax.random.fold_in(splits[6], 71), 0),
        "top_front": draw_top_front(jax.random.fold_in(splits[6], 71), 0),
        "block_map": draw_block_map(jax.random.fold_in(splits[6], 71), 0),
        "pivots": draw_pivots(jax.random.fold_in(splits[6], 71), 0),
        "noise": bell_draw(splits[4], (GROUPS, PC), 1.0, 6.0, ((0, 4),), jnp.float32),
        "top_sample": bell_draw(splits[5], (FP,), 2.0, 12.0, (), jnp.float32),
    }


HIGH = lax.Precision.HIGHEST

def eliminate(matrix, pivot_count, panel_width):
    matrix_order = matrix.shape[0]
    position = jnp.arange(matrix_order, dtype=jnp.int32)
    for panel_index in range(pivot_count // panel_width):
        first_pivot = panel_index * panel_width
        factor = jnp.linalg.cholesky(matrix[first_pivot:first_pivot + panel_width, first_pivot:first_pivot + panel_width])
        columns = lax.linalg.triangular_solve(factor, matrix[first_pivot:first_pivot + panel_width, :], left_side=True, lower=True)
        columns = jnp.where(position[None, :] >= first_pivot, columns, jnp.zeros_like(columns))
        matrix = matrix - jnp.dot(columns.T, columns, precision=HIGH)
        matrix = matrix.at[first_pivot:first_pivot + panel_width, :].set(columns)
    return matrix

def reference(child_front, top_front, block_map, pivots, noise, top_sample):
    panel_width = BS * N_COL
    top_matrix = top_front.reshape(FP, FP)
    position = jnp.arange(FC, dtype=jnp.int32)
    unit_matrix = jnp.eye(FC, dtype=top_matrix.dtype)
    offsets = jnp.arange(BS, dtype=jnp.int32)
    samples = []
    for group_index in range(GROUPS):
        child_matrix = child_front[group_index].reshape(FC, FC)
        dead_rows = (position < PC) & (position >= pivots[group_index])
        keep_mask = jnp.logical_not(dead_rows)[:, None] & jnp.logical_not(dead_rows)[None, :]
        child_matrix = jnp.where(keep_mask, child_matrix, unit_matrix)
        child_matrix = eliminate(child_matrix, PC, panel_width)
        targets = (block_map[group_index].astype(jnp.int32)[:, None] * BS + offsets[None, :]).reshape(-1).astype(jnp.int32)
        top_matrix = top_matrix.at[targets[:, None], targets[None, :]].add(child_matrix[PC:, PC:])
        coupled = top_sample[targets]
        right_side = noise[group_index] - jnp.dot(child_matrix[:PC, PC:], coupled, precision=HIGH)
        solved = lax.linalg.triangular_solve(child_matrix[:PC, :PC], right_side[:, None], left_side=True, lower=False)[:, 0]
        samples.append(solved)
    return (top_matrix.reshape(top_front.shape), jnp.stack(samples))
```

```python
import functools
import math

import jax
import jax.numpy as jnp
from jax import lax
from jax.experimental import pallas as pl
from jax.experimental.pallas import tpu as pltpu
from jax.sharding import PartitionSpec as P

MESH = pl.DeviceIdType.MESH
HIGH = lax.Precision.HIGHEST
SUB = 8
VMEM = pl.BlockSpec(memory_space=pltpu.VMEM)
SMEM = pl.BlockSpec(memory_space=pltpu.SMEM)


def split(x):
    high = x.astype(jnp.bfloat16)
    low = (x - high.astype(jnp.float32)).astype(jnp.bfloat16)
    return high, low


def dot3(left, right, dims):
    lh, ll = left
    rh, rl = right
    d = functools.partial(
        lax.dot_general, dimension_numbers=(dims, ((), ())), preferred_element_type=jnp.float32
    )
    return d(lh, rh) + (d(lh, rl) + d(ll, rh))


NN = ((1,), (0,))
TN = ((0,), (0,))
NT = ((1,), (1,))


def unit_inverse(rows_in):
    count = len(rows_in)
    width = rows_in[0].shape[1]
    strips = list(rows_in)
    lane = lax.broadcasted_iota(jnp.int32, (SUB, width), 1)
    sub = lax.broadcasted_iota(jnp.int32, (SUB, width), 0)
    result = []

    def row_of(x, i):
        return jnp.broadcast_to(x[i : i + 1, :], (SUB, width))

    for p in range(count):
        base = p * SUB
        strip = strips[p]
        cols = [
            jnp.broadcast_to(strip[:, base + j : base + j + 1], (SUB, width)) for j in range(SUB)
        ]
        scale, taps, rows = [], {}, []
        pivots = jnp.zeros((SUB, width), jnp.float32)
        for i in range(SUB):
            pivot = row_of(cols[i], i)
            recip = 1.0 / pivot
            scale.append(recip)
            pivots = jnp.where(sub == i, pivot, pivots)
            if i + 1 < SUB:
                factor = jnp.where(sub > i, cols[i] * recip, 0.0)
                for j in range(i + 1, SUB):
                    tap = row_of(cols[j], i)
                    taps[i, j] = tap
                    cols[j] = cols[j] - factor * tap
            at = lane == base + i
            row = jnp.where(at, 1.0, row_of(strip, i))
            rows.append(jnp.where((lane > base + i) & (lane < base + SUB), 0.0, row))
            if i + 1 < SUB:
                strip = jnp.where(at & (sub > i), 0.0, strip) - factor * row
        own = jnp.where(lane == base + sub, 1.0, strip)
        result.append(jnp.where(lane <= base + sub, own, 0.0) * lax.rsqrt(pivots))
        inside = (lane >= base) & (lane < base + SUB)
        for q in range(p + 1, count):
            target = strips[q]
            edge = [
                jnp.broadcast_to(target[:, base + j : base + j + 1], (SUB, width))
                for j in range(SUB)
            ]
            target = jnp.where(inside, 0.0, target)
            for i in range(SUB):
                weight = edge[i] * scale[i]
                for j in range(i + 1, SUB):
                    edge[j] = edge[j] - weight * taps[i, j]
                target = target - weight * rows[i]
            strips[q] = target
    return result


def factor_kernel(a_ref, u_ref, inv_ref):
    block = inv_ref.shape[1]
    count = a_ref.shape[0] // block
    u_ref[...] = a_ref[...]

    @pl.loop(0, count)
    def _(k):
        start = pl.multiple_of(k * block, block)
        strips = [
            u_ref[pl.ds(pl.multiple_of(start + s * SUB, SUB), SUB), pl.ds(start, block)]
            for s in range(block // SUB)
        ]
        for s, strip in enumerate(unit_inverse(strips)):
            inv_ref[pl.ds(pl.multiple_of(start + s * SUB, SUB), SUB), :] = strip

        for step in range(count - 1):

            @pl.when(k == step)
            def _():
                here, rest = step * block, (step + 1) * block
                inverse = split(inv_ref[here:rest, :])
                panel = dot3(inverse, split(u_ref[here:rest, rest:]), NN)
                u_ref[here:rest, rest:] = panel
                high, low = split(panel)
                for i in range(step + 1, count):
                    at = (i - step - 1) * block
                    left = (high[:, at : at + block], low[:, at : at + block])
                    u_ref[i * block : (i + 1) * block, i * block :] -= dot3(
                        left, (high[:, at:], low[:, at:]), TN
                    )


def solve_kernel(
    col_count, row_count, u_ref, inv_ref, near_ref, tile_ref, v_ref, noise_ref, *refs
):
    block = inv_ref.shape[1]
    pivots = u_ref.shape[0]
    count = pivots // block
    far_refs = refs[: col_count - 1]
    side_refs = refs[col_count - 1 : col_count + row_count - 2]
    mine_ref, s_ref, x_ref, w_ref, high_ref, low_ref, b_ref = refs[col_count + row_count - 2 :]
    my_col, my_row = lax.axis_index("col"), lax.axis_index("row")
    wide = near_ref.shape[1]
    for shift, piece in enumerate((near_ref, *far_refs)):
        owner = lax.rem(my_col + shift, col_count)
        for a in range(piece.shape[0] // block):
            at = pl.multiple_of((a * col_count + owner) * block, block)
            w_ref[pl.ds(at, block), :wide] = piece[a * block : (a + 1) * block, :]
    for shift, piece in enumerate((mine_ref, *side_refs)):
        owner = lax.rem(my_row + shift, row_count)
        for b in range(piece.shape[1] // block):
            at = pl.multiple_of((b * row_count + owner) * block, block)
            w_ref[pl.ds(at, block), wide:] = piece[:, b * block : (b + 1) * block].T
    rhs = v_ref[...]
    known = []
    for k in range(count):
        here, rest = k * block, (k + 1) * block
        acc = w_ref[here:rest, :]
        part = rhs[:, here:rest]
        if k:
            above = u_ref[:here, here:rest]
            acc = acc - dot3(split(above), (high_ref[:here, :], low_ref[:here, :]), TN)
            part = part - lax.dot_general(
                jnp.concatenate(known, axis=1), above, (NN, ((), ())), precision=HIGH
            )
        inverse = inv_ref[here:rest, :]
        value = dot3(split(inverse), split(acc), NN)
        high, low = split(value)
        high_ref[here:rest, :] = high
        low_ref[here:rest, :] = low
        known.append(lax.dot_general(part, inverse, (NT, ((), ())), precision=HIGH))
    s_ref[...] = tile_ref[...] - dot3(
        (high_ref[:, wide:], low_ref[:, wide:]), (high_ref[:, :wide], low_ref[:, :wide]), TN
    )
    b_ref[...] = noise_ref[...] - jnp.concatenate(known, axis=1)
    for k in reversed(range(count)):
        here, rest = k * block, (k + 1) * block
        part = b_ref[:, here:rest]
        if k + 1 < count:
            part = part - lax.dot_general(
                x_ref[:, rest:], u_ref[here:rest, rest:], (NT, ((), ())), precision=HIGH
            )
        x_ref[:, here:rest] = lax.dot_general(
            part, inv_ref[here:rest, :], (NN, ((), ())), precision=HIGH
        )


def gather_kernel(row_count, col_count, block, piece_ref, v_ref, a_ref, vs_ref, send, recv, vsend, vrecv, own):
    my_row, my_col = lax.axis_index("row"), lax.axis_index("col")
    my_group = lax.axis_index("group")
    peers = [
        (lax.rem(my_row + r, row_count), lax.rem(my_col + c, col_count))
        for r in range(row_count)
        for c in range(col_count)
        if r or c
    ]
    n_a = a_ref.shape[0] // block // col_count
    n_b = a_ref.shape[1] // block // row_count
    barrier = pltpu.get_barrier_semaphore()
    for r, c in peers:
        pl.semaphore_signal(barrier, inc=1, device_id=(my_group, r, c), device_id_type=MESH)
    pl.semaphore_wait(barrier, len(peers))

    def where(a, b):
        i = pl.multiple_of((a * col_count + my_col) * block, block)
        j = pl.multiple_of((b * row_count + my_row) * block, block)
        return a_ref.at[pl.ds(i, block), pl.ds(j, block)]

    def source(a, b):
        return piece_ref.at[a * block : (a + 1) * block, b * block : (b + 1) * block]

    slot = my_row * col_count + my_col
    copies = []
    for n, (r, c) in enumerate(peers):
        copies.append(
            pltpu.make_async_remote_copy(
                src_ref=v_ref, dst_ref=vs_ref.at[slot], send_sem=vsend.at[n],
                recv_sem=vrecv.at[n], device_id=(my_group, r, c), device_id_type=MESH,
            )
        )
    for a in range(n_a):
        for b in range(n_b):
            for n, (r, c) in enumerate(peers):
                copies.append(
                    pltpu.make_async_remote_copy(
                        src_ref=source(a, b), dst_ref=where(a, b), send_sem=send.at[n, a, b],
                        recv_sem=recv.at[n, a, b], device_id=(my_group, r, c), device_id_type=MESH,
                    )
                )
    for copy in copies:
        copy.start()
    locals_ = [pltpu.make_async_copy(v_ref, vs_ref.at[slot], own.at[n_a, 0])]
    for a in range(n_a):
        for b in range(n_b):
            locals_.append(pltpu.make_async_copy(source(a, b), where(a, b), own.at[a, b]))
    for copy in locals_:
        copy.start()
    for copy in locals_:
        copy.wait()
    for copy in copies:
        copy.wait()


def place_kernel(col_target, row_target, top_ref, arrived_ref, out_ref):
    groups, n_a, share, n_m, lanes = arrived_ref.shape
    rows = top_ref.shape[1] // share
    out_ref[...] = top_ref[...]
    for g in range(groups):
        for a in range(n_a):
            ct = col_target[g, a]
            for m in range(n_m):
                at = pl.ds(row_target[g, m], share, stride=rows)
                out_ref[ct, at, :] += arrived_ref[g, a, :, m, :]


def local(child_front, top_front, block_map, pivots, noise, top_sample):
    row_count = lax.axis_size("row")
    col_count = lax.axis_size("col")
    group_count = lax.axis_size("group")
    my_row = lax.axis_index("row")
    my_col = lax.axis_index("col")
    my_group = lax.axis_index("group")
    block = child_front.shape[3]
    pivot_total = noise.shape[1]
    child_cols = child_front.shape[1]
    child_rows = child_front.shape[4]
    tile = child_front.reshape(child_cols * block, child_rows * block)

    def global_index(blocks, stride, position):
        starts = jnp.arange(blocks, dtype=jnp.int32)[:, None] * stride + position
        return (starts * block + jnp.arange(block, dtype=jnp.int32)[None, :]).reshape(-1)

    col_index = global_index(child_cols, col_count, my_col)
    row_index = global_index(child_rows, row_count, my_row)
    live = pivots[0]
    dead_cols = (col_index < pivot_total) & (col_index >= live)
    dead_rows = (row_index < pivot_total) & (row_index >= live)
    keep = jnp.logical_not(dead_cols)[:, None] & jnp.logical_not(dead_rows)[None, :]
    unit = (col_index[:, None] == row_index[None, :]).astype(jnp.float32)
    tile = jnp.where(keep, tile, unit)
    n_col = pivot_total // col_count
    n_row = pivot_total // row_count
    pivot_blocks = pivot_total // block
    col_updates = child_cols - n_col // block
    row_updates = child_rows - n_row // block
    corner = tile[:n_col, :n_row]
    near = tile[:n_col, n_row:]
    mine = tile[n_col:, :n_row]
    last = tile[n_col:, n_row:]
    col_blocks = jnp.arange(col_updates, dtype=jnp.int32) * col_count + my_col
    row_blocks = jnp.arange(row_updates, dtype=jnp.int32) * row_count + my_row
    my_map = lax.dynamic_index_in_dim(block_map, my_group, 0, keepdims=False)
    coupled = jnp.take(
        top_sample.reshape(-1, block), jnp.take(my_map, row_blocks), axis=0
    ).reshape(-1)
    v_part = jnp.sum(near * coupled[None, :], axis=1)
    v_part = jnp.broadcast_to(v_part[None, :], (SUB, n_col))

    n_a, n_b = n_col // block, n_row // block
    peers = row_count * col_count - 1
    full, v_parts = pl.pallas_call(
        functools.partial(gather_kernel, row_count, col_count, block),
        out_shape=(
            jax.ShapeDtypeStruct((pivot_total, pivot_total), jnp.float32),
            jax.ShapeDtypeStruct((peers + 1, SUB, n_col), jnp.float32),
        ),
        in_specs=[VMEM, VMEM],
        out_specs=(VMEM, VMEM),
        scratch_shapes=[
            pltpu.SemaphoreType.DMA((peers, n_a, n_b)),
            pltpu.SemaphoreType.DMA((peers, n_a, n_b)),
            pltpu.SemaphoreType.DMA((peers,)),
            pltpu.SemaphoreType.DMA((peers,)),
            pltpu.SemaphoreType.DMA((n_a + 1, n_b)),
        ],
        compiler_params=pltpu.CompilerParams(collective_id=0, has_side_effects=True),
        name="gather",
    )(corner, v_part)
    v = v_parts.reshape(row_count, col_count, SUB, n_a, block).sum(0)
    v = v.transpose(1, 2, 0, 3).reshape(SUB, pivot_total)

    def shifted(value, axis, count, shift):
        pairs = [((i + shift) % count, i) for i in range(count)]
        return lax.ppermute(value, axis, pairs)

    far = [shifted(near, "col", col_count, s) for s in range(1, col_count)]
    side = [shifted(mine, "row", row_count, s) for s in range(1, row_count)]

    upper, inverse = pl.pallas_call(
        factor_kernel,
        out_shape=(
            jax.ShapeDtypeStruct((pivot_total, pivot_total), jnp.float32),
            jax.ShapeDtypeStruct((pivot_total, block), jnp.float32),
        ),
        in_specs=[VMEM],
        out_specs=(VMEM, VMEM),
        cost_estimate=pl.CostEstimate(
            flops=60 * pivot_total**3, bytes_accessed=8 * pivot_total**2, transcendentals=0
        ),
        name="factor",
    )(full)
    noise8 = jnp.broadcast_to(noise, (SUB, pivot_total))
    wide = near.shape[1] + mine.shape[0]
    schur, solved = pl.pallas_call(
        functools.partial(solve_kernel, col_count, row_count),
        out_shape=(
            jax.ShapeDtypeStruct(last.shape, jnp.float32),
            jax.ShapeDtypeStruct((SUB, pivot_total), jnp.float32),
        ),
        in_specs=[VMEM] * (6 + col_count - 1 + row_count - 1 + 1),
        out_specs=(VMEM, VMEM),
        scratch_shapes=[
            pltpu.VMEM((pivot_total, wide), jnp.float32),
            pltpu.VMEM((pivot_total, wide), jnp.bfloat16),
            pltpu.VMEM((pivot_total, wide), jnp.bfloat16),
            pltpu.VMEM((SUB, pivot_total), jnp.float32),
        ],
        name="forward",
    )(upper, inverse, near, last, v, noise8, *far, *side, mine)

    top_cols = top_front.shape[0]
    share = top_front.shape[3]
    top_rows = top_front.shape[4]
    shares = schur.reshape(col_updates, group_count, share, row_updates, block)
    arrived = lax.all_to_all(shares, "group", split_axis=1, concat_axis=1, tiled=True)
    arrived = arrived.reshape(col_updates, group_count, share, row_updates, block).transpose(
        1, 0, 2, 3, 4
    )
    col_target = jnp.take(block_map, col_blocks, axis=1) // col_count
    row_target = jnp.take(block_map, row_blocks, axis=1) // row_count
    top = top_front.reshape(top_cols, share * top_rows, block)
    top_out = pl.pallas_call(
        place_kernel,
        out_shape=jax.ShapeDtypeStruct(top.shape, jnp.float32),
        in_specs=[SMEM, SMEM, VMEM, VMEM],
        out_specs=VMEM,
        name="place",
    )(col_target, row_target, top, arrived)
    return (top_out.reshape(top_front.shape), solved[:1])


def solution(mesh):
    return jax.shard_map(
        local,
        mesh=mesh,
        in_specs=(
            P("group", None, "col", None, None, "row", None),
            P(None, "col", "group", None, None, "row", None),
            P(),
            P("group"),
            P("group", None),
            P(),
        ),
        out_specs=(P(None, "col", "group", None, None, "row", None), P("group", None)),
        check_vma=False,
    )
```

```python
import functools
import math

import jax
import jax.numpy as jnp
from jax import lax
from jax.experimental import pallas as pl
from jax.experimental.pallas import tpu as pltpu
from jax.sharding import PartitionSpec as P

MESH = pl.DeviceIdType.MESH
HIGH = lax.Precision.HIGHEST
SUB = 8
VMEM = pl.BlockSpec(memory_space=pltpu.VMEM)
SMEM = pl.BlockSpec(memory_space=pltpu.SMEM)


def split(x):
    high = x.astype(jnp.bfloat16)
    low = (x - high.astype(jnp.float32)).astype(jnp.bfloat16)
    return high, low


def dot3(left, right, dims):
    lh, ll = left
    rh, rl = right
    d = functools.partial(
        lax.dot_general, dimension_numbers=(dims, ((), ())), preferred_element_type=jnp.float32
    )
    return d(lh, rh) + (d(lh, rl) + d(ll, rh))


NN = ((1,), (0,))
TN = ((0,), (0,))
NT = ((1,), (1,))


def unit_inverse(rows_in):
    count = len(rows_in)
    width = rows_in[0].shape[1]
    strips = list(rows_in)
    lane = lax.broadcasted_iota(jnp.int32, (SUB, width), 1)
    sub = lax.broadcasted_iota(jnp.int32, (SUB, width), 0)
    result = []

    def row_of(x, i):
        return jnp.broadcast_to(x[i : i + 1, :], (SUB, width))

    for p in range(count):
        base = p * SUB
        strip = strips[p]
        cols = [
            jnp.broadcast_to(strip[:, base + j : base + j + 1], (SUB, width)) for j in range(SUB)
        ]
        scale, taps, rows = [], {}, []
        pivots = jnp.zeros((SUB, width), jnp.float32)
        for i in range(SUB):
            pivot = row_of(cols[i], i)
            recip = 1.0 / pivot
            scale.append(recip)
            pivots = jnp.where(sub == i, pivot, pivots)
            if i + 1 < SUB:
                factor = jnp.where(sub > i, cols[i] * recip, 0.0)
                for j in range(i + 1, SUB):
                    tap = row_of(cols[j], i)
                    taps[i, j] = tap
                    cols[j] = cols[j] - factor * tap
            at = lane == base + i
            row = jnp.where(at, 1.0, row_of(strip, i))
            rows.append(jnp.where((lane > base + i) & (lane < base + SUB), 0.0, row))
            if i + 1 < SUB:
                strip = jnp.where(at & (sub > i), 0.0, strip) - factor * row
        own = jnp.where(lane == base + sub, 1.0, strip)
        result.append(jnp.where(lane <= base + sub, own, 0.0) * lax.rsqrt(pivots))
        inside = (lane >= base) & (lane < base + SUB)
        for q in range(p + 1, count):
            target = strips[q]
            edge = [
                jnp.broadcast_to(target[:, base + j : base + j + 1], (SUB, width))
                for j in range(SUB)
            ]
            target = jnp.where(inside, 0.0, target)
            for i in range(SUB):
                weight = edge[i] * scale[i]
                for j in range(i + 1, SUB):
                    edge[j] = edge[j] - weight * taps[i, j]
                target = target - weight * rows[i]
            strips[q] = target
    return result


def factor_kernel(a_ref, u_ref, inv_ref):
    block = inv_ref.shape[1]
    count = a_ref.shape[0] // block
    for i in range(count):
        rows = slice(i * block, (i + 1) * block)
        u_ref[rows, i * block :] = a_ref[rows, i * block :]

    @pl.loop(0, count)
    def _(k):
        start = pl.multiple_of(k * block, block)
        strips = [
            u_ref[pl.ds(pl.multiple_of(start + s * SUB, SUB), SUB), pl.ds(start, block)]
            for s in range(block // SUB)
        ]
        for s, strip in enumerate(unit_inverse(strips)):
            inv_ref[pl.ds(pl.multiple_of(start + s * SUB, SUB), SUB), :] = strip

        for step in range(count - 1):

            @pl.when(k == step)
            def _():
                here, rest = step * block, (step + 1) * block
                inverse = split(inv_ref[here:rest, :])
                panel = dot3(inverse, split(u_ref[here:rest, rest:]), NN)
                u_ref[here:rest, rest:] = panel
                high, low = split(panel)
                for i in range(step + 1, count):
                    at = (i - step - 1) * block
                    left = (high[:, at : at + block], low[:, at : at + block])
                    u_ref[i * block : (i + 1) * block, i * block :] -= dot3(
                        left, (high[:, at:], low[:, at:]), TN
                    )


def solve_kernel(
    col_count, row_count, u_ref, inv_ref, near_ref, tile_ref, v_ref, noise_ref, *refs
):
    block = inv_ref.shape[1]
    pivots = u_ref.shape[0]
    count = pivots // block
    far_refs = refs[: col_count - 1]
    side_refs = refs[col_count - 1 : col_count + row_count - 2]
    mine_ref, s_ref, b_ref, w_ref, high_ref, low_ref = refs[col_count + row_count - 2 :]
    my_col, my_row = lax.axis_index("col"), lax.axis_index("row")
    wide = near_ref.shape[1]
    for shift, piece in enumerate((near_ref, *far_refs)):
        owner = lax.rem(my_col + shift, col_count)
        for a in range(piece.shape[0] // block):
            at = pl.multiple_of((a * col_count + owner) * block, block)
            w_ref[pl.ds(at, block), :wide] = piece[a * block : (a + 1) * block, :]
    for shift, piece in enumerate((mine_ref, *side_refs)):
        owner = lax.rem(my_row + shift, row_count)
        for b in range(piece.shape[1] // block):
            at = pl.multiple_of((b * row_count + owner) * block, block)
            w_ref[pl.ds(at, block), wide:] = piece[:, b * block : (b + 1) * block].T
    rhs = v_ref[...]
    known = []
    for k in range(count):
        here, rest = k * block, (k + 1) * block
        acc = w_ref[here:rest, :]
        part = rhs[:, here:rest]
        if k:
            above = u_ref[:here, here:rest]
            acc = acc - dot3(split(above), (high_ref[:here, :], low_ref[:here, :]), TN)
            part = part - lax.dot_general(
                jnp.concatenate(known, axis=1), above, (NN, ((), ())), precision=HIGH
            )
        inverse = inv_ref[here:rest, :]
        value = dot3(split(inverse), split(acc), NN)
        high, low = split(value)
        high_ref[here:rest, :] = high
        low_ref[here:rest, :] = low
        known.append(lax.dot_general(part, inverse, (NT, ((), ())), precision=HIGH))
    s_ref[...] = tile_ref[...] - dot3(
        (high_ref[:, wide:], low_ref[:, wide:]), (high_ref[:, :wide], low_ref[:, :wide]), TN
    )
    b_ref[...] = noise_ref[...] - jnp.concatenate(known, axis=1)


def flip(position, bit):
    return position + bit - 2 * bit * lax.rem(position // bit, 2)


def cube_steps(row_count, col_count, turned):
    rows = [("row", 1 << t) for t in reversed(range(row_count.bit_length() - 1))]
    cols = [("col", 1 << t) for t in reversed(range(col_count.bit_length() - 1))]
    return cols[:-1] + rows + cols[-1:] if turned else rows + cols


def gather_kernel(row_count, col_count, block, piece_ref, v_ref, a_ref, vs_ref, send, recv, own):
    my_row, my_col = lax.axis_index("row"), lax.axis_index("col")
    my_group = lax.axis_index("group")
    n_a = a_ref.shape[0] // block // col_count
    n_b = a_ref.shape[1] // block // row_count
    straight = cube_steps(row_count, col_count, False)
    turned = cube_steps(row_count, col_count, True)
    depth = len(straight)

    def moved(step, r, c):
        return (flip(r, step[1]), c) if step[0] == "row" else (r, flip(c, step[1]))

    barrier = pltpu.get_barrier_semaphore()
    for step in straight:
        r, c = moved(step, my_row, my_col)
        pl.semaphore_signal(barrier, inc=1, device_id=(my_group, r, c), device_id_type=MESH)
    pl.semaphore_wait(barrier, depth)

    parts = [
        (a, b, a * n_b + b, turned if b % 2 else straight) for a in range(n_a) for b in range(n_b)
    ]
    parts.append((None, None, n_a * n_b, straight))

    def place(part, r, c):
        a, b, n, _ = part
        if a is None:
            return vs_ref.at[r * col_count + c]
        i = pl.multiple_of((a * col_count + c) * block, block)
        j = pl.multiple_of((b * row_count + r) * block, block)
        return a_ref.at[pl.ds(i, block), pl.ds(j, block)]

    def source(part):
        a, b, n, _ = part
        if a is None:
            return v_ref
        return piece_ref.at[a * block : (a + 1) * block, b * block : (b + 1) * block]

    def guarded(part, r, c, action):
        a, b, n, _ = part
        if a is None:
            action()
        else:
            pl.when(a * col_count + c <= b * row_count + r)(action)

    def origin(part, subset):
        r, c = my_row, my_col
        for t, step in enumerate(part[3]):
            if subset >> t & 1:
                r, c = moved(step, r, c)
        return r, c

    def copy_of(part, subset, t):
        spot = place(part, *origin(part, subset))
        r, c = moved(part[3][t], my_row, my_col)
        return pltpu.make_async_remote_copy(
            src_ref=spot if subset else source(part),
            dst_ref=spot,
            send_sem=send.at[part[2], subset | 1 << t],
            recv_sem=recv.at[part[2], subset | 1 << t],
            device_id=(my_group, r, c),
            device_id_type=MESH,
        )

    def steps_after(subset):
        return range(subset.bit_length(), depth)

    def own_copy(part):
        return pltpu.make_async_copy(source(part), place(part, my_row, my_col), own.at[part[2]])

    for subset in range(1 << depth):
        for part in parts:

            def forward():
                if subset:
                    top = subset.bit_length() - 1
                    spot = place(part, *origin(part, subset))
                    r, c = moved(part[3][top], my_row, my_col)
                    pltpu.make_async_remote_copy(
                        src_ref=spot,
                        dst_ref=spot,
                        send_sem=send.at[part[2], subset],
                        recv_sem=recv.at[part[2], subset],
                        device_id=(my_group, r, c),
                        device_id_type=MESH,
                    ).wait_recv()
                for t in steps_after(subset):
                    copy_of(part, subset, t).start()
                if not subset:
                    own_copy(part).start()

            guarded(part, *origin(part, subset), forward)
    for subset in range(1 << depth):
        for part in parts:

            def finish():
                for t in steps_after(subset):
                    copy_of(part, subset, t).wait_send()
                if not subset:
                    own_copy(part).wait()

            guarded(part, *origin(part, subset), finish)


def exchange_kernel(share, s_ref, u_ref, inv_ref, b_ref, out_ref, x_ref, send, recv, own):
    block = inv_ref.shape[1]
    count = u_ref.shape[0] // block
    groups, n_a = out_ref.shape[0], out_ref.shape[1]
    my_row, my_col = lax.axis_index("row"), lax.axis_index("col")
    me = lax.axis_index("group")
    barrier = pltpu.get_barrier_semaphore()
    for d in range(1, groups):
        pl.semaphore_signal(
            barrier,
            inc=1,
            device_id=(lax.rem(me + d, groups), my_row, my_col),
            device_id_type=MESH,
        )
    pl.semaphore_wait(barrier, groups - 1)

    def source(g, a):
        at = pl.multiple_of(a * block + g * share, share)
        return s_ref.at[pl.ds(at, share), :]

    copies = []
    for d in range(1, groups):
        other = lax.rem(me + d, groups)
        for a in range(n_a):
            copies.append(
                pltpu.make_async_remote_copy(
                    src_ref=source(other, a),
                    dst_ref=out_ref.at[me, a],
                    send_sem=send.at[d, a],
                    recv_sem=recv.at[d, a],
                    device_id=(other, my_row, my_col),
                    device_id_type=MESH,
                )
            )
    for a in range(n_a):
        copies.append(pltpu.make_async_copy(source(me, a), out_ref.at[me, a], own.at[a]))
    for copy in copies:
        copy.start()
    for k in reversed(range(count)):
        here, rest = k * block, (k + 1) * block
        part = b_ref[:, here:rest]
        if k + 1 < count:
            part = part - lax.dot_general(
                x_ref[:, rest:], u_ref[here:rest, rest:], (NT, ((), ())), precision=HIGH
            )
        x_ref[:, here:rest] = lax.dot_general(
            part, inv_ref[here:rest, :], (NN, ((), ())), precision=HIGH
        )
    for copy in copies:
        copy.wait()


def place_kernel(col_count, row_count, share, map_ref, top_ref, arrived_ref, out_ref):
    groups, n_a = arrived_ref.shape[0], arrived_ref.shape[1]
    lanes = top_ref.shape[2]
    rows = top_ref.shape[1] // share
    my_row, my_col = lax.axis_index("row"), lax.axis_index("col")
    out_ref[...] = top_ref[...]
    for g in range(groups):
        for a in range(n_a):
            ct = map_ref[g, a * col_count + my_col] // col_count
            for m in range(arrived_ref.shape[3] // lanes):
                rt = map_ref[g, m * row_count + my_row] // row_count
                at = pl.ds(rt, share, stride=rows)
                out_ref[ct, at, :] += arrived_ref[g, a, :, m * lanes : (m + 1) * lanes]


def local(child_front, top_front, block_map, pivots, noise, top_sample):
    row_count = lax.axis_size("row")
    col_count = lax.axis_size("col")
    group_count = lax.axis_size("group")
    my_row = lax.axis_index("row")
    my_col = lax.axis_index("col")
    my_group = lax.axis_index("group")
    block = child_front.shape[3]
    pivot_total = noise.shape[1]
    child_cols = child_front.shape[1]
    child_rows = child_front.shape[4]
    tile = child_front.reshape(child_cols * block, child_rows * block)

    def global_index(blocks, stride, position):
        starts = jnp.arange(blocks, dtype=jnp.int32)[:, None] * stride + position
        return (starts * block + jnp.arange(block, dtype=jnp.int32)[None, :]).reshape(-1)

    col_index = global_index(child_cols, col_count, my_col)
    row_index = global_index(child_rows, row_count, my_row)
    live = pivots[0]
    dead_cols = (col_index < pivot_total) & (col_index >= live)
    dead_rows = (row_index < pivot_total) & (row_index >= live)
    keep = jnp.logical_not(dead_cols)[:, None] & jnp.logical_not(dead_rows)[None, :]
    unit = (col_index[:, None] == row_index[None, :]).astype(jnp.float32)
    tile = jnp.where(keep, tile, unit)
    n_col = pivot_total // col_count
    n_row = pivot_total // row_count
    pivot_blocks = pivot_total // block
    col_updates = child_cols - n_col // block
    row_updates = child_rows - n_row // block
    corner = tile[:n_col, :n_row]
    near = tile[:n_col, n_row:]
    mine = tile[n_col:, :n_row]
    last = tile[n_col:, n_row:]
    row_blocks = jnp.arange(row_updates, dtype=jnp.int32) * row_count + my_row
    my_map = lax.dynamic_index_in_dim(block_map, my_group, 0, keepdims=False)
    coupled = jnp.take(
        top_sample.reshape(-1, block), jnp.take(my_map, row_blocks), axis=0
    ).reshape(-1)
    v_part = jnp.sum(near * coupled[None, :], axis=1)
    v_part = jnp.broadcast_to(v_part[None, :], (SUB, n_col))

    n_a, n_b = n_col // block, n_row // block
    peers = row_count * col_count - 1
    full, v_parts = pl.pallas_call(
        functools.partial(gather_kernel, row_count, col_count, block),
        out_shape=(
            jax.ShapeDtypeStruct((pivot_total, pivot_total), jnp.float32),
            jax.ShapeDtypeStruct((peers + 1, SUB, n_col), jnp.float32),
        ),
        in_specs=[VMEM, VMEM],
        out_specs=(VMEM, VMEM),
        scratch_shapes=[
            pltpu.SemaphoreType.DMA((n_a * n_b + 1, peers + 1)),
            pltpu.SemaphoreType.DMA((n_a * n_b + 1, peers + 1)),
            pltpu.SemaphoreType.DMA((n_a * n_b + 1,)),
        ],
        compiler_params=pltpu.CompilerParams(collective_id=0, has_side_effects=True),
        name="gather",
    )(corner, v_part)
    v = v_parts.reshape(row_count, col_count, SUB, n_a, block).sum(0)
    v = v.transpose(1, 2, 0, 3).reshape(SUB, pivot_total)

    full, near_later, mine_later = lax.optimization_barrier((full, near, mine))

    def shifted(value, axis, count, shift):
        pairs = [((i + shift) % count, i) for i in range(count)]
        return lax.ppermute(value, axis, pairs)

    far = [shifted(near_later, "col", col_count, s) for s in range(1, col_count)]
    side = [shifted(mine_later, "row", row_count, s) for s in range(1, row_count)]

    upper, inverse = pl.pallas_call(
        factor_kernel,
        out_shape=(
            jax.ShapeDtypeStruct((pivot_total, pivot_total), jnp.float32),
            jax.ShapeDtypeStruct((pivot_total, block), jnp.float32),
        ),
        in_specs=[VMEM],
        out_specs=(VMEM, VMEM),
        cost_estimate=pl.CostEstimate(
            flops=60 * pivot_total**3, bytes_accessed=8 * pivot_total**2, transcendentals=0
        ),
        name="factor",
    )(full)
    noise8 = jnp.broadcast_to(noise, (SUB, pivot_total))
    wide = near.shape[1] + mine.shape[0]
    schur, rhs = pl.pallas_call(
        functools.partial(solve_kernel, col_count, row_count),
        out_shape=(
            jax.ShapeDtypeStruct(last.shape, jnp.float32),
            jax.ShapeDtypeStruct((SUB, pivot_total), jnp.float32),
        ),
        in_specs=[VMEM] * (6 + col_count - 1 + row_count - 1 + 1),
        out_specs=(VMEM, VMEM),
        scratch_shapes=[
            pltpu.VMEM((pivot_total, wide), jnp.float32),
            pltpu.VMEM((pivot_total, wide), jnp.bfloat16),
            pltpu.VMEM((pivot_total, wide), jnp.bfloat16),
        ],
        name="forward",
    )(upper, inverse, near, last, v, noise8, *far, *side, mine)

    top_cols = top_front.shape[0]
    share = top_front.shape[3]
    top_rows = top_front.shape[4]
    arrived, solved = pl.pallas_call(
        functools.partial(exchange_kernel, share),
        out_shape=(
            jax.ShapeDtypeStruct(
                (group_count, col_updates, share, row_updates * block), jnp.float32
            ),
            jax.ShapeDtypeStruct((SUB, pivot_total), jnp.float32),
        ),
        in_specs=[VMEM] * 4,
        out_specs=(VMEM, VMEM),
        scratch_shapes=[
            pltpu.SemaphoreType.DMA((group_count, col_updates)),
            pltpu.SemaphoreType.DMA((group_count, col_updates)),
            pltpu.SemaphoreType.DMA((col_updates,)),
        ],
        compiler_params=pltpu.CompilerParams(collective_id=1, has_side_effects=True),
        name="exchange",
    )(schur, upper, inverse, rhs)
    top = top_front.reshape(top_cols, share * top_rows, block)
    top_out = pl.pallas_call(
        functools.partial(place_kernel, col_count, row_count, share),
        out_shape=jax.ShapeDtypeStruct(top.shape, jnp.float32),
        in_specs=[SMEM, VMEM, VMEM],
        out_specs=VMEM,
        name="place",
    )(block_map, top, arrived)
    return (top_out.reshape(top_front.shape), solved[:1])


def solution(mesh):
    return jax.shard_map(
        local,
        mesh=mesh,
        in_specs=(
            P("group", None, "col", None, None, "row", None),
            P(None, "col", "group", None, None, "row", None),
            P(),
            P("group"),
            P("group", None),
            P(),
        ),
        out_specs=(P(None, "col", "group", None, None, "row", None), P("group", None)),
        check_vma=False,
    )
```

```python
import functools

import jax
import jax.numpy as jnp
from jax import lax
from jax.experimental import pallas as pl
from jax.experimental.pallas import tpu as pltpu
from jax.sharding import PartitionSpec as P

MESH = pl.DeviceIdType.MESH
SUB = 8
VMEM = pl.BlockSpec(memory_space=pltpu.VMEM)
SMEM = pl.BlockSpec(memory_space=pltpu.SMEM)


def split(x):
    high = x.astype(jnp.bfloat16)
    low = (x - high.astype(jnp.float32)).astype(jnp.bfloat16)
    return high, low


def dot3(left, right, dims):
    lh, ll = left
    rh, rl = right
    d = functools.partial(
        lax.dot_general, dimension_numbers=(dims, ((), ())), preferred_element_type=jnp.float32
    )
    return d(lh, rh) + (d(lh, rl) + d(ll, rh))


NN = ((1,), (0,))
TN = ((0,), (0,))
NT = ((1,), (1,))


def unit_inverse(rows_in):
    count = len(rows_in)
    width = rows_in[0].shape[1]
    strips = list(rows_in)
    lane = lax.broadcasted_iota(jnp.int32, (SUB, width), 1)
    sub = lax.broadcasted_iota(jnp.int32, (SUB, width), 0)
    result = []

    def row_of(x, i):
        return jnp.broadcast_to(x[i : i + 1, :], (SUB, width))

    for p in range(count):
        base = p * SUB
        strip = strips[p]
        cols = [
            jnp.broadcast_to(strip[:, base + j : base + j + 1], (SUB, width)) for j in range(SUB)
        ]
        scale, taps, rows = [], {}, []
        pivots = jnp.zeros((SUB, width), jnp.float32)
        for i in range(SUB):
            pivot = row_of(cols[i], i)
            recip = 1.0 / pivot
            scale.append(recip)
            pivots = jnp.where(sub == i, pivot, pivots)
            if i + 1 < SUB:
                factor = jnp.where(sub > i, cols[i] * recip, 0.0)
                for j in range(i + 1, SUB):
                    tap = row_of(cols[j], i)
                    taps[i, j] = tap
                    cols[j] = cols[j] - factor * tap
            at = lane == base + i
            row = jnp.where(at, 1.0, row_of(strip, i))
            rows.append(jnp.where((lane > base + i) & (lane < base + SUB), 0.0, row))
            if i + 1 < SUB:
                strip = jnp.where(at & (sub > i), 0.0, strip) - factor * row
        own = jnp.where(lane == base + sub, 1.0, strip)
        result.append(jnp.where(lane <= base + sub, own, 0.0) * lax.rsqrt(pivots))
        inside = (lane >= base) & (lane < base + SUB)
        for q in range(p + 1, count):
            target = strips[q]
            edge = [
                jnp.broadcast_to(target[:, base + j : base + j + 1], (SUB, width))
                for j in range(SUB)
            ]
            target = jnp.where(inside, 0.0, target)
            for i in range(SUB):
                weight = edge[i] * scale[i]
                for j in range(i + 1, SUB):
                    edge[j] = edge[j] - weight * taps[i, j]
                target = target - weight * rows[i]
            strips[q] = target
    return result


def factor_kernel(a_ref, u_ref, inv_ref):
    block = inv_ref.shape[1]
    count = a_ref.shape[0] // block
    for i in range(count):
        rows = slice(i * block, (i + 1) * block)
        u_ref[rows, i * block :] = a_ref[rows, i * block :]

    @pl.loop(0, count)
    def _(k):
        start = pl.multiple_of(k * block, block)
        strips = [
            u_ref[pl.ds(pl.multiple_of(start + s * SUB, SUB), SUB), pl.ds(start, block)]
            for s in range(block // SUB)
        ]
        for s, strip in enumerate(unit_inverse(strips)):
            inv_ref[pl.ds(pl.multiple_of(start + s * SUB, SUB), SUB), :] = strip

        for step in range(count - 1):

            @pl.when(k == step)
            def _():
                here, rest = step * block, (step + 1) * block
                inverse = split(inv_ref[here:rest, :])
                panel = dot3(inverse, split(u_ref[here:rest, rest:]), NN)
                u_ref[here:rest, rest:] = panel
                high, low = split(panel)
                for i in range(step + 1, count):
                    at = (i - step - 1) * block
                    left = (high[:, at : at + block], low[:, at : at + block])
                    u_ref[i * block : (i + 1) * block, i * block :] -= dot3(
                        left, (high[:, at:], low[:, at:]), TN
                    )


def solve_kernel(
    col_count, row_count, u_ref, inv_ref, near_ref, tile_ref, v_ref, noise_ref, *refs
):
    block = inv_ref.shape[1]
    pivots = u_ref.shape[0]
    count = pivots // block
    far_refs = refs[: col_count - 1]
    side_refs = refs[col_count - 1 : col_count + row_count - 2]
    mine_ref, s_ref, b_ref, w_ref, high_ref, low_ref = refs[col_count + row_count - 2 :]
    my_col, my_row = lax.axis_index("col"), lax.axis_index("row")
    wide = near_ref.shape[1]
    for shift, piece in enumerate((near_ref, *far_refs)):
        owner = lax.rem(my_col + shift, col_count)
        for a in range(piece.shape[0] // block):
            at = pl.multiple_of((a * col_count + owner) * block, block)
            w_ref[pl.ds(at, block), :wide] = piece[a * block : (a + 1) * block, :]
    for shift, piece in enumerate((mine_ref, *side_refs)):
        owner = lax.rem(my_row + shift, row_count)
        for b in range(piece.shape[1] // block):
            at = pl.multiple_of((b * row_count + owner) * block, block)
            w_ref[pl.ds(at, block), wide:] = piece[:, b * block : (b + 1) * block].T
    rhs = v_ref[...]
    known = []
    for k in range(count):
        here, rest = k * block, (k + 1) * block
        acc = w_ref[here:rest, :]
        part = rhs[:, here:rest]
        if k:
            above = u_ref[:here, here:rest]
            acc = acc - dot3(split(above), (high_ref[:here, :], low_ref[:here, :]), TN)
            part = part - dot3(split(jnp.concatenate(known, axis=1)), split(above), NN)
        inverse = inv_ref[here:rest, :]
        value = dot3(split(inverse), split(acc), NN)
        high, low = split(value)
        high_ref[here:rest, :] = high
        low_ref[here:rest, :] = low
        known.append(dot3(split(part), split(inverse), NT))
    s_ref[...] = tile_ref[...] - dot3(
        (high_ref[:, wide:], low_ref[:, wide:]), (high_ref[:, :wide], low_ref[:, :wide]), TN
    )
    b_ref[...] = noise_ref[...] - jnp.concatenate(known, axis=1)


def flip(position, bit):
    return position + bit - 2 * bit * lax.rem(position // bit, 2)


def cube_steps(row_count, col_count, turned):
    rows = [("row", 1 << t) for t in reversed(range(row_count.bit_length() - 1))]
    cols = [("col", 1 << t) for t in reversed(range(col_count.bit_length() - 1))]
    return cols[:-1] + rows + cols[-1:] if turned else rows + cols


def gather_kernel(row_count, col_count, block, piece_ref, v_ref, a_ref, vs_ref, send, recv, own):
    my_row, my_col = lax.axis_index("row"), lax.axis_index("col")
    my_group = lax.axis_index("group")
    n_a = a_ref.shape[0] // block // col_count
    n_b = a_ref.shape[1] // block // row_count
    straight = cube_steps(row_count, col_count, False)
    turned = cube_steps(row_count, col_count, True)
    depth = len(straight)

    def moved(step, r, c):
        return (flip(r, step[1]), c) if step[0] == "row" else (r, flip(c, step[1]))

    barrier = pltpu.get_barrier_semaphore()
    for step in straight:
        r, c = moved(step, my_row, my_col)
        pl.semaphore_signal(barrier, inc=1, device_id=(my_group, r, c), device_id_type=MESH)
    pl.semaphore_wait(barrier, depth)

    parts = [
        (a, b, a * n_b + b, turned if b % 2 else straight) for a in range(n_a) for b in range(n_b)
    ]
    parts.append((None, None, n_a * n_b, straight))

    def place(part, r, c):
        a, b, n, _ = part
        if a is None:
            return vs_ref.at[r * col_count + c]
        i = pl.multiple_of((a * col_count + c) * block, block)
        j = pl.multiple_of((b * row_count + r) * block, block)
        return a_ref.at[pl.ds(i, block), pl.ds(j, block)]

    def source(part):
        a, b, n, _ = part
        if a is None:
            return v_ref
        return piece_ref.at[a * block : (a + 1) * block, b * block : (b + 1) * block]

    def guarded(part, r, c, action):
        a, b, n, _ = part
        if a is None:
            action()
        else:
            pl.when(a * col_count + c <= b * row_count + r)(action)

    def origin(part, subset):
        r, c = my_row, my_col
        for t, step in enumerate(part[3]):
            if subset >> t & 1:
                r, c = moved(step, r, c)
        return r, c

    def copy_of(part, subset, t):
        spot = place(part, *origin(part, subset))
        r, c = moved(part[3][t], my_row, my_col)
        return pltpu.make_async_remote_copy(
            src_ref=spot if subset else source(part),
            dst_ref=spot,
            send_sem=send.at[part[2], subset | 1 << t],
            recv_sem=recv.at[part[2], subset | 1 << t],
            device_id=(my_group, r, c),
            device_id_type=MESH,
        )

    def steps_after(subset):
        return range(subset.bit_length(), depth)

    def own_copy(part):
        return pltpu.make_async_copy(source(part), place(part, my_row, my_col), own.at[part[2]])

    for subset in range(1 << depth):
        for part in parts:

            def forward():
                if subset:
                    top = subset.bit_length() - 1
                    spot = place(part, *origin(part, subset))
                    r, c = moved(part[3][top], my_row, my_col)
                    pltpu.make_async_remote_copy(
                        src_ref=spot,
                        dst_ref=spot,
                        send_sem=send.at[part[2], subset],
                        recv_sem=recv.at[part[2], subset],
                        device_id=(my_group, r, c),
                        device_id_type=MESH,
                    ).wait_recv()
                for t in steps_after(subset):
                    copy_of(part, subset, t).start()
                if not subset:
                    own_copy(part).start()

            guarded(part, *origin(part, subset), forward)
    for subset in range(1 << depth):
        for part in parts:

            def finish():
                for t in steps_after(subset):
                    copy_of(part, subset, t).wait_send()
                if not subset:
                    own_copy(part).wait()

            guarded(part, *origin(part, subset), finish)


def exchange_kernel(share, s_ref, u_ref, inv_ref, b_ref, out_ref, x_ref, send, recv, own):
    block = inv_ref.shape[1]
    count = u_ref.shape[0] // block
    groups, n_a = out_ref.shape[0], out_ref.shape[1]
    my_row, my_col = lax.axis_index("row"), lax.axis_index("col")
    me = lax.axis_index("group")
    barrier = pltpu.get_barrier_semaphore()
    for d in range(1, groups):
        pl.semaphore_signal(
            barrier,
            inc=1,
            device_id=(lax.rem(me + d, groups), my_row, my_col),
            device_id_type=MESH,
        )
    pl.semaphore_wait(barrier, groups - 1)

    def source(g, a):
        at = pl.multiple_of(a * block + g * share, share)
        return s_ref.at[pl.ds(at, share), :]

    copies = []
    for d in range(1, groups):
        other = lax.rem(me + d, groups)
        for a in range(n_a):
            copies.append(
                pltpu.make_async_remote_copy(
                    src_ref=source(other, a),
                    dst_ref=out_ref.at[me, a],
                    send_sem=send.at[d, a],
                    recv_sem=recv.at[d, a],
                    device_id=(other, my_row, my_col),
                    device_id_type=MESH,
                )
            )
    for a in range(n_a):
        copies.append(pltpu.make_async_copy(source(me, a), out_ref.at[me, a], own.at[a]))
    for copy in copies:
        copy.start()
    solved = {}
    for k in reversed(range(count)):
        here, rest = k * block, (k + 1) * block
        part = b_ref[:, here:rest]
        if k + 2 < count:
            early = jnp.concatenate([solved[n] for n in range(k + 2, count)], axis=1)
            part = part - dot3(split(early), split(u_ref[here:rest, rest + block :]), NT)
        if k + 1 < count:
            weights = split(u_ref[here:rest, rest : rest + block])
            part = part - dot3(split(solved[k + 1]), weights, NT)
        solved[k] = dot3(split(part), split(inv_ref[here:rest, :]), NN)
        x_ref[:, here:rest] = solved[k]
    for copy in copies:
        copy.wait()


def place_kernel(
    col_count, row_count, share, map_ref, top_ref, arrived_ref, sample_ref, out_ref, x_ref
):
    groups, n_a = arrived_ref.shape[0], arrived_ref.shape[1]
    lanes = top_ref.shape[2]
    rows = top_ref.shape[1] // share
    my_row, my_col = lax.axis_index("row"), lax.axis_index("col")
    here = pl.program_id(0)
    out_ref[...] = top_ref[...]
    x_ref[...] = sample_ref[:1, :]
    for g in range(groups):
        for a in range(n_a):

            @pl.when(map_ref[g, a * col_count + my_col] // col_count == here)
            def _():
                for m in range(arrived_ref.shape[3] // lanes):
                    rt = map_ref[g, m * row_count + my_row] // row_count
                    at = pl.ds(rt, share, stride=rows)
                    out_ref[0, at, :] += arrived_ref[g, a, :, m * lanes : (m + 1) * lanes]


def local(child_front, top_front, block_map, pivots, noise, top_sample):
    row_count = lax.axis_size("row")
    col_count = lax.axis_size("col")
    group_count = lax.axis_size("group")
    my_row = lax.axis_index("row")
    my_col = lax.axis_index("col")
    my_group = lax.axis_index("group")
    block = child_front.shape[3]
    pivot_total = noise.shape[1]
    child_cols = child_front.shape[1]
    child_rows = child_front.shape[4]
    tile = child_front.reshape(child_cols * block, child_rows * block)

    def global_index(blocks, stride, position):
        starts = jnp.arange(blocks, dtype=jnp.int32)[:, None] * stride + position
        return (starts * block + jnp.arange(block, dtype=jnp.int32)[None, :]).reshape(-1)

    col_index = global_index(child_cols, col_count, my_col)
    row_index = global_index(child_rows, row_count, my_row)
    live = pivots[0]
    dead_cols = (col_index < pivot_total) & (col_index >= live)
    dead_rows = (row_index < pivot_total) & (row_index >= live)
    keep = jnp.logical_not(dead_cols)[:, None] & jnp.logical_not(dead_rows)[None, :]
    unit = (col_index[:, None] == row_index[None, :]).astype(jnp.float32)
    tile = jnp.where(keep, tile, unit)
    n_col = pivot_total // col_count
    n_row = pivot_total // row_count
    pivot_blocks = pivot_total // block
    col_updates = child_cols - n_col // block
    row_updates = child_rows - n_row // block
    corner = tile[:n_col, :n_row]
    near = tile[:n_col, n_row:]
    mine = tile[n_col:, :n_row]
    last = tile[n_col:, n_row:]
    row_blocks = jnp.arange(row_updates, dtype=jnp.int32) * row_count + my_row
    my_map = lax.dynamic_index_in_dim(block_map, my_group, 0, keepdims=False)
    coupled = jnp.take(
        top_sample.reshape(-1, block), jnp.take(my_map, row_blocks), axis=0
    ).reshape(-1)
    v_part = jnp.sum(near * coupled[None, :], axis=1)
    v_part = jnp.broadcast_to(v_part[None, :], (SUB, n_col))

    n_a, n_b = n_col // block, n_row // block
    peers = row_count * col_count - 1
    full, v_parts = pl.pallas_call(
        functools.partial(gather_kernel, row_count, col_count, block),
        out_shape=(
            jax.ShapeDtypeStruct((pivot_total, pivot_total), jnp.float32),
            jax.ShapeDtypeStruct((peers + 1, SUB, n_col), jnp.float32),
        ),
        in_specs=[VMEM, VMEM],
        out_specs=(VMEM, VMEM),
        scratch_shapes=[
            pltpu.SemaphoreType.DMA((n_a * n_b + 1, peers + 1)),
            pltpu.SemaphoreType.DMA((n_a * n_b + 1, peers + 1)),
            pltpu.SemaphoreType.DMA((n_a * n_b + 1,)),
        ],
        compiler_params=pltpu.CompilerParams(collective_id=0, has_side_effects=True),
        name="gather",
    )(corner, v_part)
    v = v_parts.reshape(row_count, col_count, SUB, n_a, block).sum(0)
    v = v.transpose(1, 2, 0, 3).reshape(SUB, pivot_total)

    full, near_later, mine_later = lax.optimization_barrier((full, near, mine))

    def shifted(value, axis, count, shift):
        pairs = [((i + shift) % count, i) for i in range(count)]
        return lax.ppermute(value, axis, pairs)

    far = [shifted(near_later, "col", col_count, s) for s in range(1, col_count)]
    side = [shifted(mine_later, "row", row_count, s) for s in range(1, row_count)]

    upper, inverse = pl.pallas_call(
        factor_kernel,
        out_shape=(
            jax.ShapeDtypeStruct((pivot_total, pivot_total), jnp.float32),
            jax.ShapeDtypeStruct((pivot_total, block), jnp.float32),
        ),
        in_specs=[VMEM],
        out_specs=(VMEM, VMEM),
        cost_estimate=pl.CostEstimate(
            flops=60 * pivot_total**3, bytes_accessed=8 * pivot_total**2, transcendentals=0
        ),
        name="factor",
    )(full)
    noise8 = jnp.broadcast_to(noise, (SUB, pivot_total))
    wide = near.shape[1] + mine.shape[0]
    schur, rhs = pl.pallas_call(
        functools.partial(solve_kernel, col_count, row_count),
        out_shape=(
            jax.ShapeDtypeStruct(last.shape, jnp.float32),
            jax.ShapeDtypeStruct((SUB, pivot_total), jnp.float32),
        ),
        in_specs=[VMEM] * (6 + col_count - 1 + row_count - 1 + 1),
        out_specs=(VMEM, VMEM),
        scratch_shapes=[
            pltpu.VMEM((pivot_total, wide), jnp.float32),
            pltpu.VMEM((pivot_total, wide), jnp.bfloat16),
            pltpu.VMEM((pivot_total, wide), jnp.bfloat16),
        ],
        name="forward",
    )(upper, inverse, near, last, v, noise8, *far, *side, mine)

    top_cols = top_front.shape[0]
    share = top_front.shape[3]
    top_rows = top_front.shape[4]
    arrived, solved = pl.pallas_call(
        functools.partial(exchange_kernel, share),
        out_shape=(
            jax.ShapeDtypeStruct(
                (group_count, col_updates, share, row_updates * block), jnp.float32
            ),
            jax.ShapeDtypeStruct((SUB, pivot_total), jnp.float32),
        ),
        in_specs=[VMEM] * 4,
        out_specs=(VMEM, VMEM),
        scratch_shapes=[
            pltpu.SemaphoreType.DMA((group_count, col_updates)),
            pltpu.SemaphoreType.DMA((group_count, col_updates)),
            pltpu.SemaphoreType.DMA((col_updates,)),
        ],
        compiler_params=pltpu.CompilerParams(collective_id=1, has_side_effects=True),
        name="exchange",
    )(schur, upper, inverse, rhs)
    top = top_front.reshape(top_cols, share * top_rows, block)
    column = pl.BlockSpec((1, share * top_rows, block), lambda n: (n, 0, 0))
    top_out, sample = pl.pallas_call(
        functools.partial(place_kernel, col_count, row_count, share),
        grid=(top_cols,),
        out_shape=(
            jax.ShapeDtypeStruct(top.shape, jnp.float32),
            jax.ShapeDtypeStruct((1, pivot_total), jnp.float32),
        ),
        in_specs=[SMEM, column, VMEM, VMEM],
        out_specs=(column, VMEM),
        name="place",
    )(block_map, top, arrived, solved)
    return (top_out.reshape(top_front.shape), sample)


def solution(mesh):
    return jax.shard_map(
        local,
        mesh=mesh,
        in_specs=(
            P("group", None, "col", None, None, "row", None),
            P(None, "col", "group", None, None, "row", None),
            P(),
            P("group"),
            P("group", None),
            P(),
        ),
        out_specs=(P(None, "col", "group", None, None, "row", None), P("group", None)),
        check_vma=False,
    )
```

```python
import functools
import math

import jax
import jax.numpy as jnp
from jax import lax
from jax.experimental import pallas as pl
from jax.experimental.pallas import tpu as pltpu
from jax.sharding import PartitionSpec as P

MESH = pl.DeviceIdType.MESH
HIGH = lax.Precision.HIGHEST
SUB = 8
VMEM = pl.BlockSpec(memory_space=pltpu.VMEM)
SMEM = pl.BlockSpec(memory_space=pltpu.SMEM)


def split(x):
    high = x.astype(jnp.bfloat16)
    low = (x - high.astype(jnp.float32)).astype(jnp.bfloat16)
    return high, low


def dot3(left, right, dims):
    lh, ll = left
    rh, rl = right
    d = functools.partial(
        lax.dot_general, dimension_numbers=(dims, ((), ())), preferred_element_type=jnp.float32
    )
    return d(lh, rh) + (d(lh, rl) + d(ll, rh))


NN = ((1,), (0,))
TN = ((0,), (0,))
NT = ((1,), (1,))


def unit_inverse(rows_in):
    count = len(rows_in)
    width = rows_in[0].shape[1]
    strips = list(rows_in)
    lane = lax.broadcasted_iota(jnp.int32, (SUB, width), 1)
    sub = lax.broadcasted_iota(jnp.int32, (SUB, width), 0)
    result = []

    def row_of(x, i):
        return jnp.broadcast_to(x[i : i + 1, :], (SUB, width))

    for p in range(count):
        base = p * SUB
        strip = strips[p]
        cols = [
            jnp.broadcast_to(strip[:, base + j : base + j + 1], (SUB, width)) for j in range(SUB)
        ]
        scale, taps, rows = [], {}, []
        pivots = jnp.zeros((SUB, width), jnp.float32)
        for i in range(SUB):
            pivot = row_of(cols[i], i)
            recip = 1.0 / pivot
            scale.append(recip)
            pivots = jnp.where(sub == i, pivot, pivots)
            if i + 1 < SUB:
                factor = jnp.where(sub > i, cols[i] * recip, 0.0)
                for j in range(i + 1, SUB):
                    tap = row_of(cols[j], i)
                    taps[i, j] = tap
                    cols[j] = cols[j] - factor * tap
            at = lane == base + i
            row = jnp.where(at, 1.0, row_of(strip, i))
            rows.append(jnp.where((lane > base + i) & (lane < base + SUB), 0.0, row))
            if i + 1 < SUB:
                strip = jnp.where(at & (sub > i), 0.0, strip) - factor * row
        own = jnp.where(lane == base + sub, 1.0, strip)
        result.append(jnp.where(lane <= base + sub, own, 0.0) * lax.rsqrt(pivots))
        inside = (lane >= base) & (lane < base + SUB)
        for q in range(p + 1, count):
            target = strips[q]
            edge = [
                jnp.broadcast_to(target[:, base + j : base + j + 1], (SUB, width))
                for j in range(SUB)
            ]
            target = jnp.where(inside, 0.0, target)
            for i in range(SUB):
                weight = edge[i] * scale[i]
                for j in range(i + 1, SUB):
                    edge[j] = edge[j] - weight * taps[i, j]
                target = target - weight * rows[i]
            strips[q] = target
    return result


def factor_kernel(a_ref, u_ref, inv_ref):
    block = inv_ref.shape[1]
    count = a_ref.shape[0] // block
    for i in range(count):
        rows = slice(i * block, (i + 1) * block)
        u_ref[rows, i * block :] = a_ref[rows, i * block :]

    @pl.loop(0, count)
    def _(k):
        start = pl.multiple_of(k * block, block)
        strips = [
            u_ref[pl.ds(pl.multiple_of(start + s * SUB, SUB), SUB), pl.ds(start, block)]
            for s in range(block // SUB)
        ]
        for s, strip in enumerate(unit_inverse(strips)):
            inv_ref[pl.ds(pl.multiple_of(start + s * SUB, SUB), SUB), :] = strip

        for step in range(count - 1):

            @pl.when(k == step)
            def _():
                here, rest = step * block, (step + 1) * block
                inverse = split(inv_ref[here:rest, :])
                panel = dot3(inverse, split(u_ref[here:rest, rest:]), NN)
                u_ref[here:rest, rest:] = panel
                high, low = split(panel)
                for i in range(step + 1, count):
                    at = (i - step - 1) * block
                    left = (high[:, at : at + block], low[:, at : at + block])
                    u_ref[i * block : (i + 1) * block, i * block :] -= dot3(
                        left, (high[:, at:], low[:, at:]), TN
                    )


def solve_kernel(
    col_count, row_count, u_ref, inv_ref, near_ref, tile_ref, v_ref, noise_ref, *refs
):
    block = inv_ref.shape[1]
    pivots = u_ref.shape[0]
    count = pivots // block
    far_refs = refs[: col_count - 1]
    side_refs = refs[col_count - 1 : col_count + row_count - 2]
    mine_ref, s_ref, b_ref, w_ref, high_ref, low_ref = refs[col_count + row_count - 2 :]
    my_col, my_row = lax.axis_index("col"), lax.axis_index("row")
    wide = near_ref.shape[1]
    for shift, piece in enumerate((near_ref, *far_refs)):
        owner = lax.rem(my_col + shift, col_count)
        for a in range(piece.shape[0] // block):
            at = pl.multiple_of((a * col_count + owner) * block, block)
            w_ref[pl.ds(at, block), :wide] = piece[a * block : (a + 1) * block, :]
    for shift, piece in enumerate((mine_ref, *side_refs)):
        owner = lax.rem(my_row + shift, row_count)
        for b in range(piece.shape[1] // block):
            at = pl.multiple_of((b * row_count + owner) * block, block)
            w_ref[pl.ds(at, block), wide:] = piece[:, b * block : (b + 1) * block].T
    rhs = v_ref[...]
    known = []
    for k in range(count):
        here, rest = k * block, (k + 1) * block
        acc = w_ref[here:rest, :]
        part = rhs[:, here:rest]
        if k:
            above = u_ref[:here, here:rest]
            acc = acc - dot3(split(above), (high_ref[:here, :], low_ref[:here, :]), TN)
            part = part - lax.dot_general(
                jnp.concatenate(known, axis=1), above, (NN, ((), ())), precision=HIGH
            )
        inverse = inv_ref[here:rest, :]
        value = dot3(split(inverse), split(acc), NN)
        high, low = split(value)
        high_ref[here:rest, :] = high
        low_ref[here:rest, :] = low
        known.append(lax.dot_general(part, inverse, (NT, ((), ())), precision=HIGH))
    s_ref[...] = tile_ref[...] - dot3(
        (high_ref[:, wide:], low_ref[:, wide:]), (high_ref[:, :wide], low_ref[:, :wide]), TN
    )
    b_ref[...] = noise_ref[...] - jnp.concatenate(known, axis=1)


def flip(position, bit):
    return position + bit - 2 * bit * lax.rem(position // bit, 2)


def cube_steps(row_count, col_count, turned):
    rows = [("row", 1 << t) for t in reversed(range(row_count.bit_length() - 1))]
    cols = [("col", 1 << t) for t in reversed(range(col_count.bit_length() - 1))]
    return cols[:-1] + rows + cols[-1:] if turned else rows + cols


def gather_kernel(row_count, col_count, block, piece_ref, v_ref, a_ref, vs_ref, send, recv, own):
    my_row, my_col = lax.axis_index("row"), lax.axis_index("col")
    my_group = lax.axis_index("group")
    n_a = a_ref.shape[0] // block // col_count
    n_b = a_ref.shape[1] // block // row_count
    straight = cube_steps(row_count, col_count, False)
    turned = cube_steps(row_count, col_count, True)
    depth = len(straight)

    def moved(step, r, c):
        return (flip(r, step[1]), c) if step[0] == "row" else (r, flip(c, step[1]))

    barrier = pltpu.get_barrier_semaphore()
    for step in straight:
        r, c = moved(step, my_row, my_col)
        pl.semaphore_signal(barrier, inc=1, device_id=(my_group, r, c), device_id_type=MESH)
    pl.semaphore_wait(barrier, depth)

    parts = [
        (a, b, a * n_b + b, turned if b % 2 else straight) for a in range(n_a) for b in range(n_b)
    ]
    parts.append((None, None, n_a * n_b, straight))

    def place(part, r, c):
        a, b, n, _ = part
        if a is None:
            return vs_ref.at[r * col_count + c]
        i = pl.multiple_of((a * col_count + c) * block, block)
        j = pl.multiple_of((b * row_count + r) * block, block)
        return a_ref.at[pl.ds(i, block), pl.ds(j, block)]

    def source(part):
        a, b, n, _ = part
        if a is None:
            return v_ref
        return piece_ref.at[a * block : (a + 1) * block, b * block : (b + 1) * block]

    def guarded(part, r, c, action):
        a, b, n, _ = part
        if a is None:
            action()
        else:
            pl.when(a * col_count + c <= b * row_count + r)(action)

    def origin(part, subset):
        r, c = my_row, my_col
        for t, step in enumerate(part[3]):
            if subset >> t & 1:
                r, c = moved(step, r, c)
        return r, c

    def copy_of(part, subset, t):
        spot = place(part, *origin(part, subset))
        r, c = moved(part[3][t], my_row, my_col)
        return pltpu.make_async_remote_copy(
            src_ref=spot if subset else source(part),
            dst_ref=spot,
            send_sem=send.at[part[2], subset | 1 << t],
            recv_sem=recv.at[part[2], subset | 1 << t],
            device_id=(my_group, r, c),
            device_id_type=MESH,
        )

    def steps_after(subset):
        return range(subset.bit_length(), depth)

    def own_copy(part):
        return pltpu.make_async_copy(source(part), place(part, my_row, my_col), own.at[part[2]])

    for subset in range(1 << depth):
        for part in parts:

            def forward():
                if subset:
                    top = subset.bit_length() - 1
                    spot = place(part, *origin(part, subset))
                    r, c = moved(part[3][top], my_row, my_col)
                    pltpu.make_async_remote_copy(
                        src_ref=spot,
                        dst_ref=spot,
                        send_sem=send.at[part[2], subset],
                        recv_sem=recv.at[part[2], subset],
                        device_id=(my_group, r, c),
                        device_id_type=MESH,
                    ).wait_recv()
                for t in steps_after(subset):
                    copy_of(part, subset, t).start()
                if not subset:
                    own_copy(part).start()

            guarded(part, *origin(part, subset), forward)
    for subset in range(1 << depth):
        for part in parts:

            def finish():
                for t in steps_after(subset):
                    copy_of(part, subset, t).wait_send()
                if not subset:
                    own_copy(part).wait()

            guarded(part, *origin(part, subset), finish)


def exchange_kernel(share, s_ref, u_ref, inv_ref, b_ref, out_ref, x_ref, send, recv, own):
    block = inv_ref.shape[1]
    count = u_ref.shape[0] // block
    groups, n_a = out_ref.shape[0], out_ref.shape[1]
    my_row, my_col = lax.axis_index("row"), lax.axis_index("col")
    me = lax.axis_index("group")
    barrier = pltpu.get_barrier_semaphore()
    for d in range(1, groups):
        pl.semaphore_signal(
            barrier,
            inc=1,
            device_id=(lax.rem(me + d, groups), my_row, my_col),
            device_id_type=MESH,
        )
    pl.semaphore_wait(barrier, groups - 1)

    def source(g, a):
        at = pl.multiple_of(a * block + g * share, share)
        return s_ref.at[pl.ds(at, share), :]

    copies = []
    for d in range(1, groups):
        other = lax.rem(me + d, groups)
        for a in range(n_a):
            copies.append(
                pltpu.make_async_remote_copy(
                    src_ref=source(other, a),
                    dst_ref=out_ref.at[me, a],
                    send_sem=send.at[d, a],
                    recv_sem=recv.at[d, a],
                    device_id=(other, my_row, my_col),
                    device_id_type=MESH,
                )
            )
    for a in range(n_a):
        copies.append(pltpu.make_async_copy(source(me, a), out_ref.at[me, a], own.at[a]))
    for copy in copies:
        copy.start()
    for k in reversed(range(count)):
        here, rest = k * block, (k + 1) * block
        part = b_ref[:, here:rest]
        if k + 1 < count:
            part = part - lax.dot_general(
                x_ref[:, rest:], u_ref[here:rest, rest:], (NT, ((), ())), precision=HIGH
            )
        x_ref[:, here:rest] = lax.dot_general(
            part, inv_ref[here:rest, :], (NN, ((), ())), precision=HIGH
        )
    for copy in copies:
        copy.wait()


def place_kernel(
    col_count, row_count, share, map_ref, top_ref, arrived_ref, sample_ref, out_ref, x_ref
):
    groups, n_a = arrived_ref.shape[0], arrived_ref.shape[1]
    lanes = top_ref.shape[2]
    rows = top_ref.shape[1] // share
    my_row, my_col = lax.axis_index("row"), lax.axis_index("col")
    out_ref[...] = top_ref[...]
    x_ref[...] = sample_ref[:1, :]
    for g in range(groups):
        for a in range(n_a):
            ct = map_ref[g, a * col_count + my_col] // col_count
            for m in range(arrived_ref.shape[3] // lanes):
                rt = map_ref[g, m * row_count + my_row] // row_count
                at = pl.ds(rt, share, stride=rows)
                out_ref[ct, at, :] += arrived_ref[g, a, :, m * lanes : (m + 1) * lanes]


def local(child_front, top_front, block_map, pivots, noise, top_sample):
    row_count = lax.axis_size("row")
    col_count = lax.axis_size("col")
    group_count = lax.axis_size("group")
    my_row = lax.axis_index("row")
    my_col = lax.axis_index("col")
    my_group = lax.axis_index("group")
    block = child_front.shape[3]
    pivot_total = noise.shape[1]
    child_cols = child_front.shape[1]
    child_rows = child_front.shape[4]
    tile = child_front.reshape(child_cols * block, child_rows * block)

    def global_index(blocks, stride, position):
        starts = jnp.arange(blocks, dtype=jnp.int32)[:, None] * stride + position
        return (starts * block + jnp.arange(block, dtype=jnp.int32)[None, :]).reshape(-1)

    col_index = global_index(child_cols, col_count, my_col)
    row_index = global_index(child_rows, row_count, my_row)
    live = pivots[0]
    dead_cols = (col_index < pivot_total) & (col_index >= live)
    dead_rows = (row_index < pivot_total) & (row_index >= live)
    keep = jnp.logical_not(dead_cols)[:, None] & jnp.logical_not(dead_rows)[None, :]
    unit = (col_index[:, None] == row_index[None, :]).astype(jnp.float32)
    tile = jnp.where(keep, tile, unit)
    n_col = pivot_total // col_count
    n_row = pivot_total // row_count
    pivot_blocks = pivot_total // block
    col_updates = child_cols - n_col // block
    row_updates = child_rows - n_row // block
    corner = tile[:n_col, :n_row]
    near = tile[:n_col, n_row:]
    mine = tile[n_col:, :n_row]
    last = tile[n_col:, n_row:]
    row_blocks = jnp.arange(row_updates, dtype=jnp.int32) * row_count + my_row
    my_map = lax.dynamic_index_in_dim(block_map, my_group, 0, keepdims=False)
    coupled = jnp.take(
        top_sample.reshape(-1, block), jnp.take(my_map, row_blocks), axis=0
    ).reshape(-1)
    v_part = jnp.sum(near * coupled[None, :], axis=1)
    v_part = jnp.broadcast_to(v_part[None, :], (SUB, n_col))

    n_a, n_b = n_col // block, n_row // block
    peers = row_count * col_count - 1
    full, v_parts = pl.pallas_call(
        functools.partial(gather_kernel, row_count, col_count, block),
        out_shape=(
            jax.ShapeDtypeStruct((pivot_total, pivot_total), jnp.float32),
            jax.ShapeDtypeStruct((peers + 1, SUB, n_col), jnp.float32),
        ),
        in_specs=[VMEM, VMEM],
        out_specs=(VMEM, VMEM),
        scratch_shapes=[
            pltpu.SemaphoreType.DMA((n_a * n_b + 1, peers + 1)),
            pltpu.SemaphoreType.DMA((n_a * n_b + 1, peers + 1)),
            pltpu.SemaphoreType.DMA((n_a * n_b + 1,)),
        ],
        compiler_params=pltpu.CompilerParams(collective_id=0, has_side_effects=True),
        name="gather",
    )(corner, v_part)
    v = v_parts.reshape(row_count, col_count, SUB, n_a, block).sum(0)
    v = v.transpose(1, 2, 0, 3).reshape(SUB, pivot_total)

    full, near_later, mine_later = lax.optimization_barrier((full, near, mine))

    def shifted(value, axis, count, shift):
        pairs = [((i + shift) % count, i) for i in range(count)]
        return lax.ppermute(value, axis, pairs)

    far = [shifted(near_later, "col", col_count, s) for s in range(1, col_count)]
    side = [shifted(mine_later, "row", row_count, s) for s in range(1, row_count)]

    upper, inverse = pl.pallas_call(
        factor_kernel,
        out_shape=(
            jax.ShapeDtypeStruct((pivot_total, pivot_total), jnp.float32),
            jax.ShapeDtypeStruct((pivot_total, block), jnp.float32),
        ),
        in_specs=[VMEM],
        out_specs=(VMEM, VMEM),
        cost_estimate=pl.CostEstimate(
            flops=60 * pivot_total**3, bytes_accessed=8 * pivot_total**2, transcendentals=0
        ),
        name="factor",
    )(full)
    noise8 = jnp.broadcast_to(noise, (SUB, pivot_total))
    wide = near.shape[1] + mine.shape[0]
    schur, rhs = pl.pallas_call(
        functools.partial(solve_kernel, col_count, row_count),
        out_shape=(
            jax.ShapeDtypeStruct(last.shape, jnp.float32),
            jax.ShapeDtypeStruct((SUB, pivot_total), jnp.float32),
        ),
        in_specs=[VMEM] * (6 + col_count - 1 + row_count - 1 + 1),
        out_specs=(VMEM, VMEM),
        scratch_shapes=[
            pltpu.VMEM((pivot_total, wide), jnp.float32),
            pltpu.VMEM((pivot_total, wide), jnp.bfloat16),
            pltpu.VMEM((pivot_total, wide), jnp.bfloat16),
        ],
        name="forward",
    )(upper, inverse, near, last, v, noise8, *far, *side, mine)

    top_cols = top_front.shape[0]
    share = top_front.shape[3]
    top_rows = top_front.shape[4]
    arrived, solved = pl.pallas_call(
        functools.partial(exchange_kernel, share),
        out_shape=(
            jax.ShapeDtypeStruct(
                (group_count, col_updates, share, row_updates * block), jnp.float32
            ),
            jax.ShapeDtypeStruct((SUB, pivot_total), jnp.float32),
        ),
        in_specs=[VMEM] * 4,
        out_specs=(VMEM, VMEM),
        scratch_shapes=[
            pltpu.SemaphoreType.DMA((group_count, col_updates)),
            pltpu.SemaphoreType.DMA((group_count, col_updates)),
            pltpu.SemaphoreType.DMA((col_updates,)),
        ],
        compiler_params=pltpu.CompilerParams(collective_id=1, has_side_effects=True),
        name="exchange",
    )(schur, upper, inverse, rhs)
    top = top_front.reshape(top_cols, share * top_rows, block)
    top_out, sample = pl.pallas_call(
        functools.partial(place_kernel, col_count, row_count, share),
        out_shape=(
            jax.ShapeDtypeStruct(top.shape, jnp.float32),
            jax.ShapeDtypeStruct((1, pivot_total), jnp.float32),
        ),
        in_specs=[SMEM, VMEM, VMEM, VMEM],
        out_specs=(VMEM, VMEM),
        name="place",
    )(block_map, top, arrived, solved)
    return (top_out.reshape(top_front.shape), sample)


def solution(mesh):
    return jax.shard_map(
        local,
        mesh=mesh,
        in_specs=(
            P("group", None, "col", None, None, "row", None),
            P(None, "col", "group", None, None, "row", None),
            P(),
            P("group"),
            P("group", None),
            P(),
        ),
        out_specs=(P(None, "col", "group", None, None, "row", None), P("group", None)),
        check_vma=False,
    )
```
